512 devices in a mesh: ctx: 64 (over x, y, core), head: 8 (over z).
Axes of the slice: x: 4, y: 8, z: 8, core: 2. Of those that a mesh axis runs over, the one named last changes fastest.
Arguments:
- features: bfloat16 [32768, 8192], P(('ctx', 'head')), may hold values from -6 to 6
- input_map: bfloat16 [32768, 1024], P(('ctx', 'head')), may hold values from -6 to 6
- output_map: bfloat16 [32768, 1024], P(('ctx', 'head')), may hold values from -0.5 to 0.5
- log_decay: float32 [128, 32768], P('head', 'ctx'), may hold values from -2.3 to 0
- step_size: float32 [128, 32768], P('head', 'ctx'), may hold values from 0 to 1.25
- skip_gain: float32 [128], P('head'), may hold values from 0.5 to 2
Outputs:
- mixer_output: bfloat16 [32768, 8192], P(('ctx', 'head'))
The draws below stay inside these ranges and needn't reach their ends.
All inputs are finite; a program needn't handle non-finite values.
Results may differ from the reference program's by a relative error of at most 0.0043.
Values may be sent and summed in bfloat16 or wider, within the bound.
A program may use at most 128 MiB of HBM per device.

```python
import math
import jax
import jax.numpy as jnp
from jax import lax

HEADS = 128
HEAD_DIM = 64
STATE = 128
GROUPS = 8
BLOCK = 256
TOKENS = 32768


def decay_parts(key):
    subkeys = jax.random.split(jax.random.fold_in(key, 7), 8)
    slow_share = 0.5
    is_slow = jax.random.uniform(subkeys[0], (HEADS, 1)) < slow_share
    slow_rates = jnp.exp(jax.random.uniform(subkeys[1], (HEADS, 1), minval=math.log(3e-06), maxval=math.log(1.5e-05)))
    fast_rates = jnp.exp(jax.random.uniform(subkeys[2], (HEADS, 1), minval=math.log(0.015), maxval=math.log(0.04)))
    decay_rates = jnp.where(is_slow, slow_rates, fast_rates)
    random_perturbation = jnp.exp(jax.random.uniform(subkeys[3], (HEADS, TOKENS), minval=-0.6, maxval=0.6))
    coarse_count = TOKENS // 64 + 1
    coarse = jnp.exp(jax.random.uniform(subkeys[4], (HEADS, coarse_count), minval=-0.35, maxval=0.35))
    coarse_index = jnp.arange(TOKENS, dtype=jnp.int32) // 64
    coarse_complete = coarse[:, coarse_index]
    positions = jax.random.randint(subkeys[5], (HEADS, 3), 0, TOKENS)
    kept_entries = jax.random.uniform(subkeys[6], (HEADS, 3), minval=0.5, maxval=0.8)
    removed_entries = jnp.arange(TOKENS, dtype=jnp.int32)[None, None, :] == positions[:, :, None]
    spike_log_values = jnp.sum(jnp.where(removed_entries, jnp.log(kept_entries)[:, :, None], 0.0), axis=1)
    rate_logarithm = -decay_rates * random_perturbation * coarse_complete + spike_log_values
    return (rate_logarithm.astype(jnp.float32), subkeys[7])


def draw_log_decay(key, part):
    rate_logarithm, _ = decay_parts(key)
    return rate_logarithm


def draw_step_size(key, part):
    rate_logarithm, spare = decay_parts(key)
    spread = jax.random.uniform(spare, (HEADS, TOKENS), minval=0.8, maxval=1.2)
    return (spread * jnp.sqrt(1.0 - jnp.exp(2.0 * rate_logarithm) + 2.0 / TOKENS)).astype(jnp.float32)


def levels(own_key, extent, cuts, smallest, largest):
    factor_of = 1.0
    for position, blocks in cuts:
        draws = jax.random.uniform(jax.random.fold_in(jax.random.fold_in(own_key, 6), position), (blocks,), jnp.float32, smallest / len(cuts), largest / len(cuts))
        factor_of = factor_of * jnp.repeat(jnp.exp(draws), extent[position] // blocks).reshape((-1,) + (1,) * (len(extent) - 1 - position))
    return factor_of


def bell_draw(rng, extent, scale, reach, cuts=(), kind=jnp.bfloat16):
    array = scale * jax.random.normal(rng, extent, jnp.float32)
    if cuts:
        array = array * levels(rng, extent, cuts, -0.22, 0.18)
    return jnp.clip(array, -reach, reach).astype(kind)


def setup_inputs(seed: int = 0) -> dict:
    splits = jax.random.split(jax.random.key(seed), 7)
    return {
        "features": bell_draw(splits[0], (TOKENS, HEADS * HEAD_DIM), 1.0, 6.0, ((0, 512),)),
        "input_map": bell_draw(splits[1], (TOKENS, GROUPS * STATE), 1.0, 6.0, ((0, 512),)),
        "output_map": bell_draw(splits[2], (TOKENS, GROUPS * STATE), STATE ** -0.5, 0.5, ((0, 512),)),
        "log_decay": draw_log_decay(jax.random.fold_in(splits[6], 71), 0),
        "step_size": draw_step_size(jax.random.fold_in(splits[6], 71), 0),
        "skip_gain": jnp.clip(jnp.exp(math.log(2.0) - 1.3862944 * jax.random.uniform(splits[5], (HEADS,), jnp.float32) ** levels(splits[5], (HEADS,), ((0, 8),), -0.2, 0.2)), 0.5, 2.0),
    }


def reference(features, input_map, output_map, log_decay, step_size, skip_gain):
    per_group = HEADS // GROUPS
    group_width = per_group * HEAD_DIM
    length = features.shape[0]
    blocks = length // BLOCK
    highest = lax.Precision.HIGHEST
    rows = lax.broadcasted_iota(jnp.int32, (BLOCK, BLOCK), 0)
    cols = lax.broadcasted_iota(jnp.int32, (BLOCK, BLOCK), 1)
    causal = rows >= cols

    def one_group(group):
        slab_in = lax.dynamic_slice_in_dim(features, group * group_width, group_width, 1)
        slab_in = slab_in.reshape(blocks, BLOCK, per_group, HEAD_DIM)
        slab_write = lax.dynamic_slice_in_dim(input_map, group * STATE, STATE, 1).reshape(blocks, BLOCK, STATE)
        slab_read = lax.dynamic_slice_in_dim(output_map, group * STATE, STATE, 1).reshape(blocks, BLOCK, STATE)
        decays = lax.dynamic_slice_in_dim(log_decay, group * per_group, per_group, 0)
        decays = decays.reshape(per_group, blocks, BLOCK).transpose(1, 0, 2)
        steps = lax.dynamic_slice_in_dim(step_size, group * per_group, per_group, 0)
        steps = steps.reshape(per_group, blocks, BLOCK).transpose(1, 0, 2)
        gains = lax.dynamic_slice_in_dim(skip_gain, group * per_group, per_group, 0)

        def advance(state, item):
            block_in, block_write, block_read, block_decay, block_step = item
            running = jnp.cumsum(block_decay, axis=1)
            closing = running[:, -1]
            affinity = jnp.dot(block_read, block_write.T, preferred_element_type=jnp.float32)
            gap = jnp.where(causal[None], running[:, :, None] - running[:, None, :], 0.0)
            decay_table = jnp.where(causal[None], jnp.exp(gap), 0.0)
            weights = (affinity[None] * decay_table * block_step[:, None, :]).astype(jnp.bfloat16)
            inputs_f = block_in.astype(jnp.float32)
            diagonal = jnp.einsum('hts,shp->thp', weights.astype(jnp.float32), inputs_f, precision=highest)
            readout = jnp.einsum('tn,hnp->thp', block_read.astype(jnp.float32), state, precision=highest)
            readout = readout * jnp.exp(running).T[:, :, None]
            factor = (jnp.exp(closing[:, None] - running) * block_step).T
            scaled = (inputs_f * factor[:, :, None]).astype(jnp.bfloat16)
            fresh = jnp.einsum('tn,thp->hnp', block_write.astype(jnp.float32), scaled.astype(jnp.float32), precision=highest)
            updated = jnp.exp(closing)[:, None, None] * state + fresh
            result = diagonal + readout + gains[None, :, None] * inputs_f
            return updated, result.astype(jnp.bfloat16)

        initial = jnp.zeros((per_group, STATE, HEAD_DIM), jnp.float32)
        _, results = lax.scan(advance, initial, (slab_in, slab_write, slab_read, decays, steps))
        return results.reshape(length, group_width)

    grouped = lax.map(one_group, jnp.arange(GROUPS, dtype=jnp.int32))
    return grouped.transpose(1, 0, 2).reshape(length, HEADS * HEAD_DIM)
```

```python
import functools

import jax
import jax.numpy as jnp
from jax import lax
from jax.experimental import pallas as pl
from jax.experimental.pallas import tpu as pltpu
from jax.sharding import PartitionSpec as P

HEAD_DIM = 64
STATE = 128
BLOCK = 256
CHUNKS = 4
ROWS = 16
LANES = 128
F32 = jnp.float32
BF16 = jnp.bfloat16
MESH = pl.DeviceIdType.MESH


def kernel(
    nctx, nz,
    feat, bmap, cmap, logd, step, gain,
    out,
    rx, rb, rc, run_row, run_col, fac_col, in_col, out_col, tot, last, aff,
    sbuf, bs0, gath, dg, og, ent, ybuf, obuf,
    x_send, x_recv, b_send, b_recv, c_send, c_recv, d_send, d_recv,
    s_send, s_recv, e_send, e_recv, o_send, o_recv,
):
    ctx = lax.axis_index("ctx")
    z = lax.axis_index("head")
    rows, width = feat.shape[0], feat.shape[1] // nz
    length = rows * nz
    cw = width // CHUNKS
    heads = width // HEAD_DIM
    x_at, y_at, core = ctx // 16, lax.rem(ctx // 2, 8), lax.rem(ctx, 2)
    mine = lax.rem(x_at + y_at, CHUNKS)
    my_rows = pl.ds(pl.multiple_of((x_at * 2 + y_at // 4) * ROWS, ROWS), ROWS)
    my_lanes = pl.ds(pl.multiple_of((mine * 2 + core) * LANES, LANES), LANES)

    def wait(ref, sem):
        pltpu.make_async_copy(ref, ref, sem).wait()

    def send(src, dst, s_sem, r_sem, where):
        pltpu.make_async_remote_copy(
            src_ref=src, dst_ref=dst, send_sem=s_sem, recv_sem=r_sem,
            device_id=where, device_id_type=MESH,
        ).start()

    barrier = pltpu.get_barrier_semaphore()

    def hello_z(d, carry):
        pl.semaphore_signal(barrier, inc=1, device_id={"head": lax.rem(z + d, nz)}, device_id_type=MESH)
        return carry

    def hello_ctx(d, carry):
        pl.semaphore_signal(barrier, inc=1, device_id={"ctx": lax.rem(ctx + d, nctx)}, device_id_type=MESH)
        return carry

    lax.fori_loop(1, nz, hello_z, 0)
    lax.fori_loop(1, nctx, hello_ctx, 0)
    pl.semaphore_wait(barrier, nz + nctx - 2)

    own = pl.ds(pl.multiple_of(z * rows, rows), rows)

    def send_maps(d, carry):
        to = lax.rem(z + d, nz)
        part = pl.ds(pl.multiple_of(to * STATE, STATE), STATE)
        send(bmap.at[:, part], rb.at[own, :], b_send, b_recv, {"head": to})
        send(cmap.at[:, part], rc.at[own, :], c_send, c_recv, {"head": to})
        return carry

    def send_chunk(c):
        def go(d, carry):
            to = lax.rem(z + d, nz)
            part = pl.ds(pl.multiple_of(to * width + c * cw, cw), cw)
            send(feat.at[:, part], rx.at[own, pl.ds(c * cw, cw)], x_send, x_recv.at[c], {"head": to})
            return carry

        lax.fori_loop(1, nz, go, 0)

    lax.fori_loop(1, nz, send_maps, 0)
    for c in range(CHUNKS):
        send_chunk(c)

    rx[own, :] = feat[:, pl.ds(pl.multiple_of(z * width, width), width)]
    rb[own, :] = bmap[:, pl.ds(pl.multiple_of(z * STATE, STATE), STATE)]
    rc[own, :] = cmap[:, pl.ds(pl.multiple_of(z * STATE, STATE), STATE)]

    ti = lax.broadcasted_iota(jnp.int32, (BLOCK, BLOCK), 0)
    si = lax.broadcasted_iota(jnp.int32, (BLOCK, BLOCK), 1)
    upper = jnp.where(ti <= si, 1.0, 0.0).astype(F32)
    closings = []
    for k in range(2):
        at = slice(k * BLOCK, (k + 1) * BLOCK)
        run = jnp.dot(logd[:, at], upper, precision=lax.Precision.HIGHEST, preferred_element_type=F32)
        run_row[:, at] = run
        col = run.T
        run_col[at, :] = col
        closings.append(run[:, BLOCK - 1 : BLOCK])
        closing = col[BLOCK - 1 : BLOCK, :]
        fac_col[at, :] = jnp.exp(closing - col) * step[:, at].T
        in_col[at, :] = jnp.exp(col)
        if k == 0:
            out_col[at, :] = jnp.exp(col)
            first = closing
        else:
            out_col[at, :] = jnp.exp(col + first)
    owner = lax.broadcasted_iota(jnp.int32, (heads, width), 0)
    lane = lax.broadcasted_iota(jnp.int32, (heads, width), 1) // HEAD_DIM

    def spread(column):
        return jnp.sum(jnp.where(owner == lane, column, 0.0), axis=0, keepdims=True)

    last[...] = jnp.broadcast_to(spread(jnp.exp(closings[1])), (8, width))
    tot[...] = jnp.broadcast_to(spread(jnp.exp(closings[0] + closings[1])), (8, width))

    def place(j):
        px, py, pc = j // 16, lax.rem(j // 2, 8), lax.rem(j, 2)
        return lax.rem(px + py, CHUNKS) * 2 + pc

    def send_decay(d, carry):
        to = lax.rem(ctx + d, nctx)
        part = pl.ds(pl.multiple_of(place(to) * LANES, LANES), LANES)
        send(tot.at[:, part], dg.at[ctx], d_send, d_recv, {"ctx": to})
        return carry

    lax.fori_loop(1, nctx, send_decay, 0)
    dg[ctx] = tot[:, my_lanes]

    left = lax.broadcasted_iota(jnp.int32, (BLOCK, LANES), 1) < HEAD_DIM

    def pair_of(ref, at, h):
        return jnp.where(left, ref[at, h : h + 1], ref[at, h + 1 : h + 2])

    def wide(ref, at, c):
        h = c * cw // HEAD_DIM
        return jnp.concatenate([pair_of(ref, at, h + 2 * i) for i in range(cw // LANES)], axis=1)

    n_other = rows * (nz - 1)
    wait(rb.at[pl.ds(0, n_other), :], b_recv)
    wait(rc.at[pl.ds(0, n_other), :], c_recv)
    for k in range(2):
        at = slice(k * BLOCK, (k + 1) * BLOCK)
        aff[at, :] = lax.dot_general(
            rc[at, :], rb[at, :], (((1,), (1,)), ((), ())), preferred_element_type=F32
        )

    def states(c):
        lanes = pl.ds(c * cw, cw)
        wait(rx.at[pl.ds(0, n_other), lanes], x_recv.at[c])
        made = []
        for k in range(2):
            at = slice(k * BLOCK, (k + 1) * BLOCK)
            scaled = (rx[at, lanes].astype(F32) * wide(fac_col, at, c)).astype(BF16)
            made.append(
                lax.dot_general(rb[at, :], scaled, (((0,), (0,)), ((), ())), preferred_element_type=F32)
            )
        sbuf[:, lanes] = (last[0:1, lanes] * made[0] + made[1]).astype(BF16)
        bs0[:, lanes] = made[0].astype(BF16)

        def go(i, carry):
            q = lax.rem(i + ctx, 16)
            tx, th, tc = q // 4, lax.rem(q // 2, 2), lax.rem(q, 2)
            to = tx * 16 + (th * 4 + lax.rem(c - tx + 4, 4)) * 2 + tc

            @pl.when(to != ctx)
            def _():
                send(
                    sbuf.at[
                        pl.ds(pl.multiple_of((tx * 2 + th) * ROWS, ROWS), ROWS),
                        pl.ds(pl.multiple_of((c * 2 + tc) * LANES, LANES), LANES),
                    ],
                    gath.at[ctx], s_send, s_recv, {"ctx": to},
                )

            return carry

        lax.fori_loop(0, 16, go, 0)

    def scan(c):
        @pl.when(mine == c)
        def _():
            gath[ctx] = sbuf[my_rows, my_lanes]
            wait(dg.at[pl.ds(0, nctx - 1)], d_recv)
            wait(gath.at[pl.ds(0, nctx - 1)], s_recv)

            def hop(i, before):
                og[i] = before.astype(BF16)
                decay = dg[i]
                return jnp.concatenate([decay, decay], axis=0) * before + gath[i].astype(F32)

            lax.fori_loop(0, nctx, hop, jnp.zeros((ROWS, LANES), F32))
            ent[my_rows, my_lanes] = og[ctx]

            def go(d, carry):
                to = lax.rem(ctx + d, nctx)
                send(og.at[to], ent.at[my_rows, my_lanes], e_send, e_recv.at[c], {"ctx": to})
                return carry

            lax.fori_loop(1, nctx, go, 0)

    def inside(c):
        def block(k, carry):
            at = pl.ds(pl.multiple_of(k * BLOCK, BLOCK), BLOCK)
            causal = ti >= si
            for i in range(cw // LANES):
                h = c * cw // HEAD_DIM + 2 * i
                lanes = pl.ds(c * cw + i * LANES, LANES)
                xs = rx[at, lanes]
                parts = []
                for j in (h, h + 1):
                    gap = jnp.where(causal, run_col[at, j : j + 1] - run_row[j : j + 1, at], -1e30)
                    weight = (aff[at, :] * jnp.exp(gap) * step[j : j + 1, at]).astype(BF16)
                    parts.append(jnp.dot(weight, xs, preferred_element_type=F32))
                total = jnp.where(left, parts[0], parts[1])
                ybuf[at, lanes] = total + jnp.where(left, gain[h], gain[h + 1]) * xs.astype(F32)

                @pl.when(k == 1)
                def _():
                    read = jnp.dot(rc[at, :], bs0[:, lanes], preferred_element_type=F32)
                    ybuf[at, lanes] += pair_of(in_col, at, h) * read

            return carry

        lax.fori_loop(0, 2, block, 0)

    def finish(c):
        lanes = pl.ds(c * cw, cw)

        @pl.when(mine == c)
        def _():
            wait(og.at[pl.ds(0, 15)], e_recv.at[c])

        @pl.when(mine != c)
        def _():
            wait(og.at[pl.ds(0, 16)], e_recv.at[c])

        for k in range(2):
            at = slice(k * BLOCK, (k + 1) * BLOCK)
            read = jnp.dot(rc[at, :], ent[:, lanes], preferred_element_type=F32)
            obuf[at, lanes] = (ybuf[at, lanes] + wide(out_col, at, c) * read).astype(BF16)
        there = pl.ds(pl.multiple_of(z * width + c * cw, cw), cw)

        def go(d, carry):
            to = lax.rem(z + d, nz)
            send(
                obuf.at[pl.ds(pl.multiple_of(to * rows, rows), rows), lanes],
                out.at[:, there], o_send, o_recv, {"head": to},
            )
            return carry

        lax.fori_loop(1, nz, go, 0)
        out[:, there] = obuf[own, lanes]

    states(0)
    inside(0)
    states(1)
    scan(0)
    inside(1)
    states(2)
    scan(1)
    finish(0)
    inside(2)
    states(3)
    scan(2)
    finish(1)
    inside(3)
    scan(3)
    finish(2)
    finish(3)

    wait(rx.at[pl.ds(0, n_other), :], x_send)
    wait(rb.at[pl.ds(0, n_other), :], b_send)
    wait(rc.at[pl.ds(0, n_other), :], c_send)
    wait(dg.at[pl.ds(0, nctx - 1)], d_send)
    wait(gath.at[pl.ds(0, nctx - 1)], s_send)
    wait(og.at[pl.ds(0, nctx - 1)], e_send)
    wait(obuf.at[pl.ds(0, n_other), :], o_send)
    wait(obuf.at[pl.ds(0, n_other), :], o_recv)


def solution(mesh):
    nctx, nz = mesh.shape["ctx"], mesh.shape["head"]

    def per_device(features, input_map, output_map, log_decay, step_size, skip_gain):
        rows, total = features.shape
        width = total // nz
        length = rows * nz
        heads = width // HEAD_DIM
        vm = pl.BlockSpec(memory_space=pltpu.VMEM)
        dma = pltpu.SemaphoreType.DMA
        return pl.pallas_call(
            functools.partial(kernel, nctx, nz),
            name="mixer",
            out_shape=jax.ShapeDtypeStruct((rows, total), BF16),
            in_specs=[vm, vm, vm, vm, vm, pl.BlockSpec(memory_space=pltpu.SMEM)],
            out_specs=vm,
            scratch_shapes=[
                pltpu.VMEM((length, width), BF16),
                pltpu.VMEM((length, STATE), BF16),
                pltpu.VMEM((length, STATE), BF16),
                pltpu.VMEM((heads, length), F32),
                pltpu.VMEM((length, heads), F32),
                pltpu.VMEM((length, heads), F32),
                pltpu.VMEM((length, heads), F32),
                pltpu.VMEM((length, heads), F32),
                pltpu.VMEM((8, width), F32),
                pltpu.VMEM((8, width), F32),
                pltpu.VMEM((length, BLOCK), F32),
                pltpu.VMEM((STATE, width), BF16),
                pltpu.VMEM((STATE, width), BF16),
                pltpu.VMEM((nctx, ROWS, LANES), BF16),
                pltpu.VMEM((nctx, 8, LANES), F32),
                pltpu.VMEM((nctx, ROWS, LANES), BF16),
                pltpu.VMEM((STATE, width), BF16),
                pltpu.VMEM((length, width), F32),
                pltpu.VMEM((length, width), BF16),
                dma, dma((CHUNKS,)), dma, dma, dma, dma, dma, dma,
                dma, dma, dma, dma((CHUNKS,)), dma, dma,
            ],
            compiler_params=pltpu.CompilerParams(
                collective_id=0, has_side_effects=True, vmem_limit_bytes=40 * 1024 * 1024
            ),
        )(features, input_map, output_map, log_decay, step_size, skip_gain)

    placed = (
        P(("ctx", "head"), None),
        P(("ctx", "head"), None),
        P(("ctx", "head"), None),
        P("head", "ctx"),
        P("head", "ctx"),
        P("head"),
    )
    return jax.shard_map(
        per_device, mesh=mesh, in_specs=placed, out_specs=P(("ctx", "head"), None), check_vma=False
    )
```

```python
import functools

import jax
import jax.numpy as jnp
from jax import lax
from jax.experimental import pallas as pl
from jax.experimental.pallas import tpu as pltpu
from jax.sharding import PartitionSpec as P

HEAD_DIM = 64
STATE = 128
BLOCK = 256
CHUNKS = 4
ROWS = 16
LANES = 128
F32 = jnp.float32
BF16 = jnp.bfloat16
MESH = pl.DeviceIdType.MESH


def kernel(
    nctx, nz,
    feat, bmap, cmap, logd_in, step_in, gain_in,
    out,
    logd, step, gain, load,
    rx, rb, rc, run_row, run_col, fac_col, in_col, out_col, tot, last, aff,
    sbuf, bs0, gath, dg, og, ent, ybuf, obuf,
    x_send, x_recv, b_send, b_recv, c_send, c_recv, d_send, d_recv,
    s_send, s_recv, e_send, e_recv, o_send, o_recv, column, ready, keep,
):
    ctx = lax.axis_index("ctx")
    z = lax.axis_index("head")
    rows, width = feat.shape[0], feat.shape[1] // nz
    length = rows * nz
    cw = width // CHUNKS
    heads = width // HEAD_DIM
    x_at, y_at, core = ctx // 16, lax.rem(ctx // 2, 8), lax.rem(ctx, 2)
    mine = lax.rem(x_at + y_at, CHUNKS)
    my_rows = pl.ds(pl.multiple_of((x_at * 2 + y_at // 4) * ROWS, ROWS), ROWS)
    my_lanes = pl.ds(pl.multiple_of((mine * 2 + core) * LANES, LANES), LANES)

    def wait(ref, sem):
        pltpu.make_async_copy(ref, ref, sem).wait()

    def send(src, dst, s_sem, r_sem, where):
        pltpu.make_async_remote_copy(
            src_ref=src, dst_ref=dst, send_sem=s_sem, recv_sem=r_sem,
            device_id=where, device_id_type=MESH,
        ).start()

    def far_first(i):
        half = (i + 1) // 2
        return jnp.where(lax.rem(i, 2) == 1, nz // 2 - half, nz // 2 + half)

    own = pl.ds(pl.multiple_of(z * rows, rows), rows)

    def fetch(src, dst, i):
        copy = pltpu.make_async_copy(src, dst, load.at[i])
        copy.start()
        return copy

    small = [fetch(logd_in, logd, 0), fetch(step_in, step, 1), fetch(gain_in, gain, 2)]
    kept = [
        fetch(feat.at[:, pl.ds(pl.multiple_of(z * width, width), width)], rx.at[own, :], 3),
        fetch(bmap.at[:, pl.ds(pl.multiple_of(z * STATE, STATE), STATE)], rb.at[own, :], 4),
        fetch(cmap.at[:, pl.ds(pl.multiple_of(z * STATE, STATE), STATE)], rc.at[own, :], 5),
    ]
    barrier = pltpu.get_barrier_semaphore()

    def hello_z(d, carry):
        pl.semaphore_signal(barrier, inc=1, device_id={"head": lax.rem(z + d, nz)}, device_id_type=MESH)
        return carry

    def hello_ctx(d, carry):
        pl.semaphore_signal(barrier, inc=1, device_id={"ctx": lax.rem(ctx + d, nctx)}, device_id_type=MESH)
        return carry

    def hello_plane(d, carry):
        pl.semaphore_signal(
            column, inc=1, device_id={"ctx": lax.rem(ctx + d, nctx)}, device_id_type=MESH
        )
        return carry

    def hello_ready(d, carry):
        pl.semaphore_signal(
            ready, inc=1, device_id={"head": lax.rem(z + d, nz)}, device_id_type=MESH
        )
        return carry

    lax.fori_loop(1, nz, hello_z, 0)

    @pl.when(z == 0)
    def _():
        lax.fori_loop(1, nctx, hello_ctx, 0)

    pl.semaphore_wait(barrier, jnp.where(z == 0, nz + nctx - 2, nz - 1))

    def send_maps(d, carry):
        to = lax.rem(z + far_first(d), nz)
        part = pl.ds(pl.multiple_of(to * STATE, STATE), STATE)
        send(bmap.at[:, part], rb.at[own, :], b_send, b_recv, {"head": to})
        send(cmap.at[:, part], rc.at[own, :], c_send, c_recv, {"head": to})
        return carry

    def send_chunk(c):
        def go(d, carry):
            to = lax.rem(z + far_first(d), nz)
            part = pl.ds(pl.multiple_of(to * width + c * cw, cw), cw)
            send(feat.at[:, part], rx.at[own, pl.ds(c * cw, cw)], x_send, x_recv.at[c], {"head": to})
            return carry

        lax.fori_loop(0, nz - 1, go, 0)

    lax.fori_loop(0, nz - 1, send_maps, 0)
    for c in range(CHUNKS):
        send_chunk(c)

    @pl.when(z == 0)
    def _():
        lax.fori_loop(1, nctx, hello_plane, 0)

    for copy in small:
        copy.wait()

    ti = lax.broadcasted_iota(jnp.int32, (BLOCK, BLOCK), 0)
    si = lax.broadcasted_iota(jnp.int32, (BLOCK, BLOCK), 1)
    upper = jnp.where(ti <= si, 1.0, 0.0).astype(F32)
    closings = []
    for k in range(2):
        at = slice(k * BLOCK, (k + 1) * BLOCK)
        run = jnp.dot(logd[:, at], upper, precision=lax.Precision.HIGHEST, preferred_element_type=F32)
        run_row[:, at] = run
        col = run.T
        run_col[at, :] = col
        closings.append(run[:, BLOCK - 1 : BLOCK])
        closing = col[BLOCK - 1 : BLOCK, :]
        fac_col[at, :] = jnp.exp(closing - col) * step[:, at].T
        in_col[at, :] = jnp.exp(col)
        if k == 0:
            out_col[at, :] = jnp.exp(col)
            first = closing
        else:
            out_col[at, :] = jnp.exp(col + first)
    owner = lax.broadcasted_iota(jnp.int32, (heads, width), 0)
    lane = lax.broadcasted_iota(jnp.int32, (heads, width), 1) // HEAD_DIM

    def spread(column):
        return jnp.sum(jnp.where(owner == lane, column, 0.0), axis=0, keepdims=True)

    last[...] = jnp.broadcast_to(spread(jnp.exp(closings[1])), (8, width))
    tot[...] = jnp.broadcast_to(spread(jnp.exp(closings[0] + closings[1])), (8, width))

    def place(j):
        px, py, pc = j // 16, lax.rem(j // 2, 8), lax.rem(j, 2)
        return lax.rem(px + py, CHUNKS) * 2 + pc

    def send_decay(d, carry):
        to = lax.rem(ctx + d, nctx)
        part = pl.ds(pl.multiple_of(place(to) * LANES, LANES), LANES)
        send(tot.at[:, part], dg.at[ctx], d_send, d_recv, {"ctx": to})
        return carry

    dg[ctx] = tot[:, my_lanes]

    left = lax.broadcasted_iota(jnp.int32, (BLOCK, LANES), 1) < HEAD_DIM

    def pair_of(ref, at, h):
        return jnp.where(left, ref[at, h : h + 1], ref[at, h + 1 : h + 2])

    def wide(ref, at, c):
        h = c * cw // HEAD_DIM
        return jnp.concatenate([pair_of(ref, at, h + 2 * i) for i in range(cw // LANES)], axis=1)

    n_other = rows * (nz - 1)
    for copy in kept:
        copy.wait()
    wait(rb.at[pl.ds(0, n_other), :], b_recv)
    wait(rc.at[pl.ds(0, n_other), :], c_recv)
    for k in range(2):
        at = slice(k * BLOCK, (k + 1) * BLOCK)
        aff[at, :] = lax.dot_general(
            rc[at, :], rb[at, :], (((1,), (1,)), ((), ())), preferred_element_type=F32
        )

    @pl.when(z == 0)
    def _():
        pl.semaphore_wait(column, nctx - 1)
        lax.fori_loop(1, nz, hello_ready, 0)

    @pl.when(z != 0)
    def _():
        pl.semaphore_wait(ready, 1)

    lax.fori_loop(1, nctx, send_decay, 0)

    def states(c):
        lanes = pl.ds(c * cw, cw)
        wait(rx.at[pl.ds(0, n_other), lanes], x_recv.at[c])
        made = []
        for k in range(2):
            at = slice(k * BLOCK, (k + 1) * BLOCK)
            scaled = (rx[at, lanes].astype(F32) * wide(fac_col, at, c)).astype(BF16)
            made.append(
                lax.dot_general(rb[at, :], scaled, (((0,), (0,)), ((), ())), preferred_element_type=F32)
            )
        sbuf[:, lanes] = (last[0:1, lanes] * made[0] + made[1]).astype(BF16)
        bs0[:, lanes] = made[0].astype(BF16)

        def go(i, carry):
            q = lax.rem(i + ctx, 16)
            tx, th, tc = q // 4, lax.rem(q // 2, 2), lax.rem(q, 2)
            to = tx * 16 + (th * 4 + lax.rem(c - tx + 4, 4)) * 2 + tc

            @pl.when(to != ctx)
            def _():
                send(
                    sbuf.at[
                        pl.ds(pl.multiple_of((tx * 2 + th) * ROWS, ROWS), ROWS),
                        pl.ds(pl.multiple_of((c * 2 + tc) * LANES, LANES), LANES),
                    ],
                    gath.at[ctx], s_send, s_recv, {"ctx": to},
                )

            return carry

        lax.fori_loop(0, 16, go, 0)

    def scan(c):
        @pl.when(mine == c)
        def _():
            gath[ctx] = sbuf[my_rows, my_lanes]
            wait(dg.at[pl.ds(0, nctx - 1)], d_recv)
            wait(gath.at[pl.ds(0, nctx - 1)], s_recv)

            def hop(i, before):
                og[i] = before.astype(BF16)
                decay = dg[i]
                return jnp.concatenate([decay, decay], axis=0) * before + gath[i].astype(F32)

            lax.fori_loop(0, nctx, hop, jnp.zeros((ROWS, LANES), F32))
            ent[my_rows, my_lanes] = og[ctx]

            def go(d, carry):
                to = lax.rem(ctx + d, nctx)
                send(og.at[to], ent.at[my_rows, my_lanes], e_send, e_recv.at[c], {"ctx": to})
                return carry

            lax.fori_loop(1, nctx, go, 0)

    def inside(c):
        def block(k, carry):
            at = pl.ds(pl.multiple_of(k * BLOCK, BLOCK), BLOCK)
            causal = ti >= si
            for i in range(cw // LANES):
                h = c * cw // HEAD_DIM + 2 * i
                lanes = pl.ds(c * cw + i * LANES, LANES)
                xs = rx[at, lanes]
                parts = []
                for j in (h, h + 1):
                    gap = jnp.where(causal, run_col[at, j : j + 1] - run_row[j : j + 1, at], -1e30)
                    weight = (aff[at, :] * jnp.exp(gap) * step[j : j + 1, at]).astype(BF16)
                    parts.append(jnp.dot(weight, xs, preferred_element_type=F32))
                total = jnp.where(left, parts[0], parts[1])
                ybuf[at, lanes] = total + jnp.where(left, gain[h], gain[h + 1]) * xs.astype(F32)

                @pl.when(k == 1)
                def _():
                    read = jnp.dot(rc[at, :], bs0[:, lanes], preferred_element_type=F32)
                    ybuf[at, lanes] += pair_of(in_col, at, h) * read

            return carry

        lax.fori_loop(0, 2, block, 0)

    def finish(c):
        lanes = pl.ds(c * cw, cw)

        @pl.when(mine == c)
        def _():
            wait(og.at[pl.ds(0, 15)], e_recv.at[c])

        @pl.when(mine != c)
        def _():
            wait(og.at[pl.ds(0, 16)], e_recv.at[c])

        for k in range(2):
            at = slice(k * BLOCK, (k + 1) * BLOCK)
            read = jnp.dot(rc[at, :], ent[:, lanes], preferred_element_type=F32)
            obuf[at, lanes] = (ybuf[at, lanes] + wide(out_col, at, c) * read).astype(BF16)
        there = pl.ds(pl.multiple_of(z * width + c * cw, cw), cw)

        def go(d, carry):
            to = lax.rem(z + far_first(d), nz)
            send(
                obuf.at[pl.ds(pl.multiple_of(to * rows, rows), rows), lanes],
                out.at[:, there], o_send, o_recv, {"head": to},
            )
            return carry

        lax.fori_loop(0, nz - 1, go, 0)
        pltpu.make_async_copy(obuf.at[own, lanes], out.at[:, there], keep).start()

    states(0)
    inside(0)
    states(1)
    scan(0)
    inside(1)
    states(2)
    scan(1)
    inside(2)
    finish(0)
    states(3)
    scan(2)
    inside(3)
    finish(1)
    scan(3)
    finish(2)
    finish(3)

    wait(rx.at[pl.ds(0, n_other), :], x_send)
    wait(rb.at[pl.ds(0, n_other), :], b_send)
    wait(rc.at[pl.ds(0, n_other), :], c_send)
    wait(dg.at[pl.ds(0, nctx - 1)], d_send)
    wait(gath.at[pl.ds(0, nctx - 1)], s_send)
    wait(og.at[pl.ds(0, nctx - 1)], e_send)
    wait(obuf.at[pl.ds(0, n_other), :], o_send)
    wait(obuf.at[pl.ds(0, n_other), :], o_recv)
    wait(obuf.at[own, :], keep)


def solution(mesh):
    nctx, nz = mesh.shape["ctx"], mesh.shape["head"]

    def per_device(features, input_map, output_map, log_decay, step_size, skip_gain):
        rows, total = features.shape
        width = total // nz
        length = rows * nz
        heads = width // HEAD_DIM
        vm = pl.BlockSpec(memory_space=pltpu.VMEM)
        dma = pltpu.SemaphoreType.DMA
        return pl.pallas_call(
            functools.partial(kernel, nctx, nz),
            name="mixer",
            out_shape=jax.ShapeDtypeStruct((rows, total), BF16),
            in_specs=[pl.BlockSpec(memory_space=pltpu.HBM)] * 6,
            out_specs=pl.BlockSpec(memory_space=pltpu.HBM),
            scratch_shapes=[
                pltpu.VMEM((heads, length), F32),
                pltpu.VMEM((heads, length), F32),
                pltpu.SMEM((heads,), F32),
                dma((6,)),
                pltpu.VMEM((length, width), BF16),
                pltpu.VMEM((length, STATE), BF16),
                pltpu.VMEM((length, STATE), BF16),
                pltpu.VMEM((heads, length), F32),
                pltpu.VMEM((length, heads), F32),
                pltpu.VMEM((length, heads), F32),
                pltpu.VMEM((length, heads), F32),
                pltpu.VMEM((length, heads), F32),
                pltpu.VMEM((8, width), F32),
                pltpu.VMEM((8, width), F32),
                pltpu.VMEM((length, BLOCK), F32),
                pltpu.VMEM((STATE, width), BF16),
                pltpu.VMEM((STATE, width), BF16),
                pltpu.VMEM((nctx, ROWS, LANES), BF16),
                pltpu.VMEM((nctx, 8, LANES), F32),
                pltpu.VMEM((nctx, ROWS, LANES), BF16),
                pltpu.VMEM((STATE, width), BF16),
                pltpu.VMEM((length, width), F32),
                pltpu.VMEM((length, width), BF16),
                dma, dma((CHUNKS,)), dma, dma, dma, dma, dma, dma,
                dma, dma, dma, dma((CHUNKS,)), dma, dma,
                pltpu.SemaphoreType.REGULAR, pltpu.SemaphoreType.REGULAR, dma,
            ],
            compiler_params=pltpu.CompilerParams(
                collective_id=0, has_side_effects=True, vmem_limit_bytes=63 * 1024 * 1024
            ),
        )(features, input_map, output_map, log_decay, step_size, skip_gain)

    placed = (
        P(("ctx", "head"), None),
        P(("ctx", "head"), None),
        P(("ctx", "head"), None),
        P("head", "ctx"),
        P("head", "ctx"),
        P("head"),
    )
    return jax.shard_map(
        per_device, mesh=mesh, in_specs=placed, out_specs=P(("ctx", "head"), None), check_vma=False
    )
```

```python
import functools

import jax
import jax.numpy as jnp
from jax import lax
from jax.experimental import pallas as pl
from jax.experimental.pallas import tpu as pltpu
from jax.sharding import PartitionSpec as P

HEAD_DIM = 64
STATE = 128
BLOCK = 256
CHUNKS = 8
ROWS = 16
LANES = 128
F32 = jnp.float32
BF16 = jnp.bfloat16
MESH = pl.DeviceIdType.MESH


def kernel(
    nctx, nz,
    feat, bmap, cmap, logd_in, step_in, gain_in,
    out,
    logd, step, gain, load,
    rx, rb, rc, run_row, run_col, fac_col, in_col, out_col, tot, last, aff,
    sbuf, bs0, gath, dg, og, ent, ybuf, obuf,
    x_send, x_recv, b_send, b_recv, c_send, c_recv, d_send, d_recv,
    s_send, s_recv, e_send, e_recv, o_send, o_recv, column, ready, keep,
):
    ctx = lax.axis_index("ctx")
    z = lax.axis_index("head")
    rows, width = feat.shape[0], feat.shape[1] // nz
    length = rows * nz
    cw = width // CHUNKS
    heads = width // HEAD_DIM
    x_at, y_at, core = ctx // 16, lax.rem(ctx // 2, 8), lax.rem(ctx, 2)
    mine = lax.rem(x_at + y_at, 4) * 2 + core
    my_rows = pl.ds(pl.multiple_of((x_at * 2 + y_at // 4) * ROWS, ROWS), ROWS)
    my_lanes = pl.ds(pl.multiple_of(mine * LANES, LANES), LANES)

    def wait(ref, sem):
        pltpu.make_async_copy(ref, ref, sem).wait()

    def send(src, dst, s_sem, r_sem, where):
        pltpu.make_async_remote_copy(
            src_ref=src, dst_ref=dst, send_sem=s_sem, recv_sem=r_sem,
            device_id=where, device_id_type=MESH,
        ).start()

    def far_first(i):
        half = (i + 1) // 2
        return jnp.where(lax.rem(i, 2) == 1, nz // 2 - half, nz // 2 + half)

    own = pl.ds(pl.multiple_of(z * rows, rows), rows)

    def fetch(src, dst, i):
        copy = pltpu.make_async_copy(src, dst, load.at[i])
        copy.start()
        return copy

    small = [fetch(logd_in, logd, 0), fetch(step_in, step, 1), fetch(gain_in, gain, 2)]
    kept = [
        fetch(feat.at[:, pl.ds(pl.multiple_of(z * width, width), width)], rx.at[own, :], 3),
        fetch(bmap.at[:, pl.ds(pl.multiple_of(z * STATE, STATE), STATE)], rb.at[own, :], 4),
        fetch(cmap.at[:, pl.ds(pl.multiple_of(z * STATE, STATE), STATE)], rc.at[own, :], 5),
    ]
    barrier = pltpu.get_barrier_semaphore()

    def hello_z(d, carry):
        pl.semaphore_signal(barrier, inc=1, device_id={"head": lax.rem(z + d, nz)}, device_id_type=MESH)
        return carry

    def hello_ctx(d, carry):
        pl.semaphore_signal(barrier, inc=1, device_id={"ctx": lax.rem(ctx + d, nctx)}, device_id_type=MESH)
        return carry

    def hello_plane(d, carry):
        pl.semaphore_signal(
            column, inc=1, device_id={"ctx": lax.rem(ctx + d, nctx)}, device_id_type=MESH
        )
        return carry

    def hello_ready(d, carry):
        pl.semaphore_signal(
            ready, inc=1, device_id={"head": lax.rem(z + d, nz)}, device_id_type=MESH
        )
        return carry

    lax.fori_loop(1, nz, hello_z, 0)

    @pl.when(z == 0)
    def _():
        lax.fori_loop(1, nctx, hello_ctx, 0)

    pl.semaphore_wait(barrier, jnp.where(z == 0, nz + nctx - 2, nz - 1))

    def send_maps(d, carry):
        to = lax.rem(z + far_first(d), nz)
        part = pl.ds(pl.multiple_of(to * STATE, STATE), STATE)
        send(bmap.at[:, part], rb.at[own, :], b_send, b_recv, {"head": to})
        send(cmap.at[:, part], rc.at[own, :], c_send, c_recv, {"head": to})
        return carry

    def send_chunk(c):
        def go(d, carry):
            to = lax.rem(z + far_first(d), nz)
            part = pl.ds(pl.multiple_of(to * width + c * cw, cw), cw)
            send(feat.at[:, part], rx.at[own, pl.ds(c * cw, cw)], x_send, x_recv.at[c], {"head": to})
            return carry

        lax.fori_loop(0, nz - 1, go, 0)

    lax.fori_loop(0, nz - 1, send_maps, 0)
    for c in range(CHUNKS):
        send_chunk(c)

    @pl.when(z == 0)
    def _():
        lax.fori_loop(1, nctx, hello_plane, 0)

    for copy in small:
        copy.wait()

    ti = lax.broadcasted_iota(jnp.int32, (BLOCK, BLOCK), 0)
    si = lax.broadcasted_iota(jnp.int32, (BLOCK, BLOCK), 1)
    upper = jnp.where(ti <= si, 1.0, 0.0).astype(F32)
    closings = []
    for k in range(2):
        at = slice(k * BLOCK, (k + 1) * BLOCK)
        run = jnp.dot(logd[:, at], upper, precision=lax.Precision.HIGHEST, preferred_element_type=F32)
        run_row[:, at] = run
        col = run.T
        run_col[at, :] = col
        closings.append(run[:, BLOCK - 1 : BLOCK])
        closing = col[BLOCK - 1 : BLOCK, :]
        fac_col[at, :] = jnp.exp(closing - col) * step[:, at].T
        in_col[at, :] = jnp.exp(col)
        if k == 0:
            out_col[at, :] = jnp.exp(col)
            first = closing
        else:
            out_col[at, :] = jnp.exp(col + first)
    owner = lax.broadcasted_iota(jnp.int32, (heads, width), 0)
    lane = lax.broadcasted_iota(jnp.int32, (heads, width), 1) // HEAD_DIM

    def spread(column):
        return jnp.sum(jnp.where(owner == lane, column, 0.0), axis=0, keepdims=True)

    last[...] = jnp.broadcast_to(spread(jnp.exp(closings[1])), (8, width))
    tot[...] = jnp.broadcast_to(spread(jnp.exp(closings[0] + closings[1])), (8, width))

    def place(j):
        px, py, pc = j // 16, lax.rem(j // 2, 8), lax.rem(j, 2)
        return lax.rem(px + py, 4) * 2 + pc

    def send_decay(d, carry):
        to = lax.rem(ctx + d, nctx)
        part = pl.ds(pl.multiple_of(place(to) * LANES, LANES), LANES)
        send(tot.at[:, part], dg.at[ctx], d_send, d_recv, {"ctx": to})
        return carry

    dg[ctx] = tot[:, my_lanes]

    left = lax.broadcasted_iota(jnp.int32, (BLOCK, LANES), 1) < HEAD_DIM

    def pair_of(ref, at, h):
        return jnp.where(left, ref[at, h : h + 1], ref[at, h + 1 : h + 2])

    def wide(ref, at, c):
        h = c * cw // HEAD_DIM
        return jnp.concatenate([pair_of(ref, at, h + 2 * i) for i in range(cw // LANES)], axis=1)

    n_other = rows * (nz - 1)
    for copy in kept:
        copy.wait()
    wait(rb.at[pl.ds(0, n_other), :], b_recv)
    wait(rc.at[pl.ds(0, n_other), :], c_recv)
    for k in range(2):
        at = slice(k * BLOCK, (k + 1) * BLOCK)
        aff[at, :] = lax.dot_general(
            rc[at, :], rb[at, :], (((1,), (1,)), ((), ())), preferred_element_type=F32
        )

    @pl.when(z == 0)
    def _():
        pl.semaphore_wait(column, nctx - 1)
        lax.fori_loop(1, nz, hello_ready, 0)

    @pl.when(z != 0)
    def _():
        pl.semaphore_wait(ready, 1)

    lax.fori_loop(1, nctx, send_decay, 0)

    def states(c):
        lanes = pl.ds(c * cw, cw)
        wait(rx.at[pl.ds(0, n_other), lanes], x_recv.at[c])
        made = []
        for k in range(2):
            at = slice(k * BLOCK, (k + 1) * BLOCK)
            scaled = (rx[at, lanes].astype(F32) * wide(fac_col, at, c)).astype(BF16)
            made.append(
                lax.dot_general(rb[at, :], scaled, (((0,), (0,)), ((), ())), preferred_element_type=F32)
            )
        sbuf[:, lanes] = (last[0:1, lanes] * made[0] + made[1]).astype(BF16)
        bs0[:, lanes] = made[0].astype(BF16)

        def go(i, carry):
            q = lax.rem(i + ctx, 8)
            tx, th = q // 2, lax.rem(q, 2)
            to = tx * 16 + (th * 4 + lax.rem(c // 2 - tx + 4, 4)) * 2 + c % 2

            @pl.when(to != ctx)
            def _():
                send(
                    sbuf.at[
                        pl.ds(pl.multiple_of((tx * 2 + th) * ROWS, ROWS), ROWS),
                        pl.ds(c * LANES, LANES),
                    ],
                    gath.at[ctx], s_send, s_recv, {"ctx": to},
                )

            return carry

        lax.fori_loop(0, 8, go, 0)

    def scan(c):
        @pl.when(mine == c)
        def _():
            gath[ctx] = sbuf[my_rows, my_lanes]
            wait(dg.at[pl.ds(0, nctx - 1)], d_recv)
            wait(gath.at[pl.ds(0, nctx - 1)], s_recv)

            def hop(i, before):
                og[i] = before.astype(BF16)
                decay = dg[i]
                return jnp.concatenate([decay, decay], axis=0) * before + gath[i].astype(F32)

            lax.fori_loop(0, nctx, hop, jnp.zeros((ROWS, LANES), F32))
            ent[my_rows, my_lanes] = og[ctx]

            def go(d, carry):
                to = lax.rem(ctx + d, nctx)
                send(og.at[to], ent.at[my_rows, my_lanes], e_send, e_recv.at[c], {"ctx": to})
                return carry

            lax.fori_loop(1, nctx, go, 0)

    def inside(c):
        def block(k, carry):
            at = pl.ds(pl.multiple_of(k * BLOCK, BLOCK), BLOCK)
            causal = ti >= si
            for i in range(cw // LANES):
                h = c * cw // HEAD_DIM + 2 * i
                lanes = pl.ds(c * cw + i * LANES, LANES)
                xs = rx[at, lanes]
                parts = []
                for j in (h, h + 1):
                    gap = jnp.where(causal, run_col[at, j : j + 1] - run_row[j : j + 1, at], -1e30)
                    weight = (aff[at, :] * jnp.exp(gap) * step[j : j + 1, at]).astype(BF16)
                    parts.append(jnp.dot(weight, xs, preferred_element_type=F32))
                total = jnp.where(left, parts[0], parts[1])
                ybuf[at, lanes] = total + jnp.where(left, gain[h], gain[h + 1]) * xs.astype(F32)

                @pl.when(k == 1)
                def _():
                    read = jnp.dot(rc[at, :], bs0[:, lanes], preferred_element_type=F32)
                    ybuf[at, lanes] += pair_of(in_col, at, h) * read

            return carry

        lax.fori_loop(0, 2, block, 0)

    def finish(c):
        lanes = pl.ds(c * cw, cw)

        @pl.when(mine == c)
        def _():
            wait(og.at[pl.ds(0, 7)], e_recv.at[c])

        @pl.when(mine != c)
        def _():
            wait(og.at[pl.ds(0, 8)], e_recv.at[c])

        for k in range(2):
            at = slice(k * BLOCK, (k + 1) * BLOCK)
            read = jnp.dot(rc[at, :], ent[:, lanes], preferred_element_type=F32)
            obuf[at, lanes] = (ybuf[at, lanes] + wide(out_col, at, c) * read).astype(BF16)
        there = pl.ds(pl.multiple_of(z * width + c * cw, cw), cw)

        def go(d, carry):
            to = lax.rem(z + far_first(d), nz)
            send(
                obuf.at[pl.ds(pl.multiple_of(to * rows, rows), rows), lanes],
                out.at[:, there], o_send, o_recv, {"head": to},
            )
            return carry

        lax.fori_loop(0, nz - 1, go, 0)
        pltpu.make_async_copy(obuf.at[own, lanes], out.at[:, there], keep).start()

    states(0)
    inside(0)
    states(1)
    inside(1)
    states(2)
    scan(0)
    inside(2)
    states(3)
    scan(1)
    inside(3)
    states(4)
    scan(2)
    inside(4)
    finish(0)
    states(5)
    scan(3)
    inside(5)
    finish(1)
    states(6)
    scan(4)
    inside(6)
    finish(2)
    states(7)
    scan(5)
    inside(7)
    finish(3)
    scan(6)
    finish(4)
    scan(7)
    finish(5)
    finish(6)
    finish(7)

    wait(rx.at[pl.ds(0, n_other), :], x_send)
    wait(rb.at[pl.ds(0, n_other), :], b_send)
    wait(rc.at[pl.ds(0, n_other), :], c_send)
    wait(dg.at[pl.ds(0, nctx - 1)], d_send)
    wait(gath.at[pl.ds(0, nctx - 1)], s_send)
    wait(og.at[pl.ds(0, nctx - 1)], e_send)
    wait(obuf.at[pl.ds(0, n_other), :], o_send)
    wait(obuf.at[pl.ds(0, n_other), :], o_recv)
    wait(obuf.at[own, :], keep)


def solution(mesh):
    nctx, nz = mesh.shape["ctx"], mesh.shape["head"]

    def per_device(features, input_map, output_map, log_decay, step_size, skip_gain):
        rows, total = features.shape
        width = total // nz
        length = rows * nz
        heads = width // HEAD_DIM
        vm = pl.BlockSpec(memory_space=pltpu.VMEM)
        dma = pltpu.SemaphoreType.DMA
        return pl.pallas_call(
            functools.partial(kernel, nctx, nz),
            name="mixer",
            out_shape=jax.ShapeDtypeStruct((rows, total), BF16),
            in_specs=[pl.BlockSpec(memory_space=pltpu.HBM)] * 6,
            out_specs=pl.BlockSpec(memory_space=pltpu.HBM),
            scratch_shapes=[
                pltpu.VMEM((heads, length), F32),
                pltpu.VMEM((heads, length), F32),
                pltpu.SMEM((heads,), F32),
                dma((6,)),
                pltpu.VMEM((length, width), BF16),
                pltpu.VMEM((length, STATE), BF16),
                pltpu.VMEM((length, STATE), BF16),
                pltpu.VMEM((heads, length), F32),
                pltpu.VMEM((length, heads), F32),
                pltpu.VMEM((length, heads), F32),
                pltpu.VMEM((length, heads), F32),
                pltpu.VMEM((length, heads), F32),
                pltpu.VMEM((8, width), F32),
                pltpu.VMEM((8, width), F32),
                pltpu.VMEM((length, BLOCK), F32),
                pltpu.VMEM((STATE, width), BF16),
                pltpu.VMEM((STATE, width), BF16),
                pltpu.VMEM((nctx, ROWS, LANES), BF16),
                pltpu.VMEM((nctx, 8, LANES), F32),
                pltpu.VMEM((nctx, ROWS, LANES), BF16),
                pltpu.VMEM((STATE, width), BF16),
                pltpu.VMEM((length, width), F32),
                pltpu.VMEM((length, width), BF16),
                dma, dma((CHUNKS,)), dma, dma, dma, dma, dma, dma,
                dma, dma, dma, dma((CHUNKS,)), dma, dma,
                pltpu.SemaphoreType.REGULAR, pltpu.SemaphoreType.REGULAR, dma,
            ],
            compiler_params=pltpu.CompilerParams(
                collective_id=0, has_side_effects=True, vmem_limit_bytes=63 * 1024 * 1024
            ),
        )(features, input_map, output_map, log_decay, step_size, skip_gain)

    placed = (
        P(("ctx", "head"), None),
        P(("ctx", "head"), None),
        P(("ctx", "head"), None),
        P("head", "ctx"),
        P("head", "ctx"),
        P("head"),
    )
    return jax.shard_map(
        per_device, mesh=mesh, in_specs=placed, out_specs=P(("ctx", "head"), None), check_vma=False
    )
```
